32 devices in a mesh: blk: 8 (over z, y), grp: 4 (over x, core).
Axes of the slice: x: 2, y: 2, z: 4, core: 2. Of those that a mesh axis runs over, the one named last changes fastest.
Arguments:
- state: float32 [6, 131072], P(None, ('blk', 'grp')), may hold values from -6 to 6
- mass: float32 [131072], P(('blk', 'grp')), may hold values from 1.5258789e-06 to 3.8146973e-05
- active_index: int32 [8, 32], P('blk'), may hold values from 0 to 16383, as said below
- counts: int32 [8], P('blk'), may hold values from 8 to 32, as said below
Outputs:
- acc_jerk: float32 [6, 256], P(None, 'blk')
- potential: float32 [256], P('blk')
The draws below stay inside these ranges and needn't reach their ends.
Inputs may be any that keep to these rules, and one draw needn't show every extreme that they name: `active_index`: each row holds 32 different star numbers of its slot block; only the first counts[b] entries of row b are active. `counts`: in every draw some slot is full, with 32 active stars.
All inputs are finite; a program needn't handle non-finite values.
Results may differ from the reference program's by a relative error of at most 0.0003.
Values sent between devices are 32-bit elements; how exact they have to be, the bound alone decides.
A program may use at most 64 MiB of HBM per device.

```python
import math
import jax
import jax.numpy as jnp
from jax import lax

F_DEV = 4096
CAP = 32
STARS = 131072
N_BLK = 8
N_GRP = 4


def draw_active_index(key, part):
    keys = jax.random.split(key, N_BLK)
    rows = jax.vmap(lambda single: jax.random.permutation(single, F_DEV * N_GRP)[:CAP])(keys)
    return rows.astype(jnp.int32)


def draw_counts(key, part):
    base = jax.random.randint(key, (N_BLK,), CAP // 4, CAP + 1)
    chosen = jax.random.randint(jax.random.fold_in(key, 7), (), 0, N_BLK)
    return jnp.where(jnp.arange(N_BLK) == chosen, CAP, base).astype(jnp.int32)


def levels(own_key, dims, pieces, smallest, high):
    def one(dim, parts):
        steps = jax.random.uniform(jax.random.fold_in(jax.random.fold_in(own_key, 6), dim), (parts,), jnp.float32, smallest / len(pieces), high / len(pieces))
        return jnp.repeat(jnp.exp(steps), dims[dim] // parts).reshape((-1,) + (1,) * (len(dims) - dim - 1))

    level = one(*pieces[0])
    for cut in pieces[1:]:
        level = level * one(*cut)
    return level


def normal_values(key, extent, scale, limit, pieces=(), held_as=jnp.bfloat16):
    gain = levels(key, extent, pieces, -0.22, 0.18) if pieces else 1.0
    drawn = jax.random.normal(key, extent, jnp.float32) * scale * gain
    return jnp.minimum(jnp.maximum(drawn, -limit), limit).astype(held_as)


def setup_inputs(seed: int = 0) -> dict:
    arg_keys = jax.random.split(jax.random.key(seed), 5)
    state = normal_values(arg_keys[0], (6, STARS), 1.0, 6.0, ((1, 32),), jnp.float32)
    mass = jnp.clip(jnp.exp(math.log(3.814697265625e-05) - 3.218876 * jax.random.uniform(arg_keys[1], (STARS,), jnp.float32) ** levels(arg_keys[1], (STARS,), ((0, 32),), -0.2, 0.2)), 1.5258789289873675e-06, 3.814697265625e-05)
    active_index = draw_active_index(jax.random.fold_in(arg_keys[4], 71), 0)
    counts = draw_counts(jax.random.fold_in(arg_keys[4], 71), 0)
    return dict(state=state, mass=mass, active_index=active_index, counts=counts)


softening = 0.001

def pair_terms(active, field):
    dpos = field[0:3, None, :] - active[0:3, :, None]
    dvel = field[3:6, None, :] - active[3:6, :, None]
    raw = lax.optimization_barrier(jnp.sum(dpos * dpos, axis=0))
    weight = jnp.where(raw == 0.0, 0.0, field[6][None, :])
    inv = lax.rsqrt(raw + softening)
    first = weight * inv
    third = first * inv * inv
    along = lax.optimization_barrier(jnp.sum(dpos * dvel, axis=0))
    fifth = 3.0 * along * third * inv * inv
    accel = lax.optimization_barrier(jnp.sum(third[None] * dpos, axis=-1))
    jerk = lax.optimization_barrier(jnp.sum(third[None] * dvel - fifth[None] * dpos, axis=-1))
    pot = -lax.optimization_barrier(jnp.sum(first, axis=-1))
    return jnp.concatenate([accel, jerk, pot[None]], axis=0)

def reference(state, mass, active_index, counts):
    slot_size = F_DEV * N_GRP
    offsets = jnp.arange(N_BLK, dtype=jnp.int32)[:, None] * slot_size
    global_ids = (active_index + offsets).astype(jnp.int32).reshape(-1)
    active = jnp.take(state, global_ids, axis=1)
    slots = jnp.transpose(active.reshape(6, N_BLK, CAP), (1, 0, 2))
    field = jnp.concatenate([state, mass[None, :]], axis=0)
    blocks = jnp.transpose(field.reshape(7, N_BLK, slot_size), (1, 0, 2))

    def one_slot(rows):

        def add_block(total, block):
            return (total + pair_terms(rows, block), None)
        total, unused = lax.scan(add_block, jnp.zeros((7, CAP), state.dtype), blocks)
        return total
    terms = lax.map(one_slot, slots)
    live = jnp.arange(CAP, dtype=jnp.int32)[None, :] < counts[:, None]
    terms = jnp.where(live[:, None, :], terms, 0.0)
    flat = jnp.transpose(terms, (1, 0, 2)).reshape(7, N_BLK * CAP)
    return (flat[0:6], flat[6])
```

```python
import functools

import jax
import jax.numpy as jnp
from jax import lax
from jax.experimental import pallas as pl
from jax.experimental.pallas import tpu as pltpu
from jax.sharding import PartitionSpec as P

softening = 0.001
LANES = 128
MESH = pl.DeviceIdType.MESH
UNROLL = 4


def spread_chunk(state_ref, mass_ref, wide_ref, chunk):
    start = pl.multiple_of(chunk * LANES, LANES)
    rows = jnp.concatenate(
        [state_ref[:, pl.ds(start, LANES)], mass_ref[pl.ds(chunk, 1), :], jnp.zeros((1, LANES), jnp.float32)], axis=0
    )
    columns = rows.T
    for c in range(7):
        wide_ref[c, pl.ds(start, LANES), :] = jnp.broadcast_to(columns[:, c : c + 1], (LANES, LANES))


def tile_terms(active, wide_ref, stars):
    mine = [jnp.broadcast_to(active[c : c + 1, :], (8, LANES)) for c in range(6)]

    def body(step, totals):
        totals = list(totals)
        for u in range(UNROLL):
            at = pl.ds(pl.multiple_of((step * UNROLL + u) * 8, 8), 8)
            dx = [wide_ref[c, at, :] - mine[c] for c in range(3)]
            dv = [wide_ref[c, at, :] - mine[c] for c in range(3, 6)]
            raw = dx[0] * dx[0] + dx[1] * dx[1] + dx[2] * dx[2]
            weight = jnp.where(raw == 0.0, 0.0, wide_ref[6, at, :])
            inv = lax.rsqrt(raw + softening)
            square = inv * inv
            first = weight * inv
            third = first * square
            along = dx[0] * dv[0] + dx[1] * dv[1] + dx[2] * dv[2]
            ratio = (3.0 * along) * square
            for c in range(3):
                totals[c] = totals[c] + third * dx[c]
                totals[3 + c] = totals[3 + c] + third * (dv[c] - ratio * dx[c])
            totals[6] = totals[6] + first
        return tuple(totals)

    zero = jnp.zeros((8, LANES), jnp.float32)
    totals = lax.fori_loop(0, stars // (8 * UNROLL), body, (zero,) * 7)
    sums = [jnp.sum(t, axis=0, keepdims=True) for t in totals]
    return jnp.concatenate(sums[:6] + [-sums[6], jnp.zeros((1, LANES), jnp.float32)], axis=0)


def kernel(
    n_blk, n_grp, cap, state_ref, mass_ref, picks_ref, counts_ref, out_ref, pot_ref,
    wide_ref, part_ref, part_in, own_ref, own_in, sum_ref, sum_in, tot_ref, tot_in,
    part_s, part_r, own_s, own_r, sum_s, sum_r, tot_s, tot_r,
):
    blk, grp = lax.axis_index("blk"), lax.axis_index("grp")
    stars = state_ref.shape[1]
    size = LANES // cap
    tiles = n_blk // size
    tile, place = blk // size, blk % size
    hops = [(dt, dr) for dt in range(tiles) for dr in range(size)]

    def slot(dt, dr):
        return ((tile + dt) % tiles) * size + (place + dr) % size

    barrier = pltpu.get_barrier_semaphore()
    for d in range(1, n_grp):
        pl.semaphore_signal(barrier, inc=1, device_id=(blk, (grp + d) % n_grp), device_id_type=MESH)
    for dt, dr in hops[1:]:
        pl.semaphore_signal(barrier, inc=1, device_id=(slot(dt, dr), grp), device_id_type=MESH)

    picks = jnp.concatenate([picks_ref[...] - grp * stars] * size, axis=1)
    lane = lax.broadcasted_iota(jnp.int32, (1, LANES), 1)
    picks = jnp.where(lane // cap == place, picks, -1)
    depth = 512
    row = lax.broadcasted_iota(jnp.int32, (depth, LANES), 0)
    found = jnp.zeros((6, LANES), jnp.float32)
    for k in range(stars // depth):
        hot = jnp.where(row + k * depth == picks, 1.0, 0.0).astype(jnp.bfloat16)
        rest = state_ref[:, k * depth : (k + 1) * depth]
        for _ in range(3):
            piece = rest.astype(jnp.bfloat16)
            rest = rest - piece.astype(jnp.float32)
            found = found + jnp.dot(piece, hot, preferred_element_type=jnp.float32)
    part_ref[...] = jnp.concatenate([found, jnp.zeros((2, LANES), jnp.float32)], axis=0)

    pl.semaphore_wait(barrier, n_grp - 1 + n_blk - 1)

    def grp_copy(src, dst, send, recv, d):
        return pltpu.make_async_remote_copy(
            src_ref=src, dst_ref=dst.at[d - 1], send_sem=send.at[d - 1], recv_sem=recv.at[d - 1],
            device_id=(blk, (grp + d) % n_grp), device_id_type=MESH,
        )

    parts = [grp_copy(part_ref, part_in, part_s, part_r, d) for d in range(1, n_grp)]
    for copy in parts:
        copy.start()

    chunks = stars // LANES

    @pl.loop(0, chunks // 2)
    def _(chunk):
        spread_chunk(state_ref, mass_ref, wide_ref, chunk)

    own = part_ref[...]
    for d, copy in enumerate(parts):
        copy.wait_recv()
        own = own + part_in[d]
    own_ref[...] = own

    shares = {}
    for dt, dr in hops[1:]:
        shares[dt, dr] = pltpu.make_async_remote_copy(
            src_ref=own_ref, dst_ref=own_in.at[dt * size + dr], send_sem=own_s.at[dt * size + dr],
            recv_sem=own_r.at[dt * size + dr], device_id=(slot(dt, dr), grp), device_id_type=MESH,
        )
        shares[dt, dr].start()

    @pl.loop(chunks // 2, chunks)
    def _(chunk):
        spread_chunk(state_ref, mass_ref, wide_ref, chunk)

    results = {}
    for dt in range(tiles):
        active = own if dt == 0 else None
        for dr in range(size):
            if (dt, dr) != (0, 0):
                shares[dt, dr].wait_recv()
                got = own_in[dt * size + dr]
                active = got if active is None else active + got
        terms = tile_terms(active, wide_ref, stars)
        sum_ref[dt] = terms
        for dr in range(size):
            if (dt, dr) != (0, 0):
                results[dt, dr] = pltpu.make_async_remote_copy(
                    src_ref=sum_ref.at[dt], dst_ref=sum_in.at[dt * size + dr], send_sem=sum_s.at[dt * size + dr],
                    recv_sem=sum_r.at[dt * size + dr], device_id=(slot(tiles - dt, dr), grp), device_id_type=MESH,
                )
                results[dt, dr].start()

    total = sum_ref[0]
    for dt, dr in hops[1:]:
        results[dt, dr].wait_recv()
        total = total + sum_in[dt * size + dr]
    tot_ref[...] = total
    totals = [grp_copy(tot_ref, tot_in, tot_s, tot_r, d) for d in range(1, n_grp)]
    for copy in totals:
        copy.start()
    for d, copy in enumerate(totals):
        copy.wait_recv()
        total = total + tot_in[d]

    total = pltpu.roll(total, ((size - place) % size) * cap, 1)
    total = jnp.where(lane < counts_ref[0], total, 0.0)
    out_ref[...] = total[0:6, 0:cap]
    pot_ref[...] = total[6:7, 0:cap]

    for copy in parts + list(shares.values()) + list(results.values()) + totals:
        copy.wait_send()


def solution(mesh):
    n_blk, n_grp = mesh.shape["blk"], mesh.shape["grp"]

    def on_device(state, mass, active_index, counts):
        stars, cap = state.shape[1], active_index.shape[1]
        f32 = jnp.float32
        tile = (8, LANES)
        sems = pltpu.SemaphoreType.DMA
        vmem = pl.BlockSpec(memory_space=pltpu.VMEM)
        out, pot = pl.pallas_call(
            functools.partial(kernel, n_blk, n_grp, cap),
            out_shape=(jax.ShapeDtypeStruct((6, cap), f32), jax.ShapeDtypeStruct((1, cap), f32)),
            in_specs=[vmem, vmem, vmem, pl.BlockSpec(memory_space=pltpu.SMEM)],
            out_specs=(vmem, vmem),
            scratch_shapes=[
                pltpu.VMEM((7, stars, LANES), f32),
                pltpu.VMEM(tile, f32),
                pltpu.VMEM((n_grp - 1, *tile), f32),
                pltpu.VMEM(tile, f32),
                pltpu.VMEM((n_blk, *tile), f32),
                pltpu.VMEM((n_blk * cap // LANES, *tile), f32),
                pltpu.VMEM((n_blk, *tile), f32),
                pltpu.VMEM(tile, f32),
                pltpu.VMEM((n_grp - 1, *tile), f32),
                sems((n_grp - 1,)), sems((n_grp - 1,)),
                sems((n_blk,)), sems((n_blk,)),
                sems((n_blk,)), sems((n_blk,)),
                sems((n_grp - 1,)), sems((n_grp - 1,)),
            ],
            compiler_params=pltpu.CompilerParams(
                collective_id=0, has_side_effects=True, vmem_limit_bytes=40 * 1024 * 1024
            ),
        )(state, mass.reshape(stars // LANES, LANES), active_index, counts)
        return out, pot.reshape(cap)

    placed = (P(None, ("blk", "grp")), P(("blk", "grp")), P("blk", None), P("blk"))
    return jax.shard_map(
        on_device, mesh=mesh, in_specs=placed, out_specs=(P(None, "blk"), P("blk")), check_vma=False
    )
```

```python
import functools

import jax
import jax.numpy as jnp
from jax import lax
from jax.experimental import pallas as pl
from jax.experimental.pallas import tpu as pltpu
from jax.sharding import PartitionSpec as P

softening = 0.001
LANES = 128
MESH = pl.DeviceIdType.MESH
UNROLL = 8
SPREAD = 512


def pieces(rows):
    out = []
    for _ in range(3):
        piece = rows.astype(jnp.bfloat16).astype(jnp.float32)
        out.append(piece)
        rows = rows - piece
    return jnp.concatenate(out, axis=0)


def spread_chunk(state_ref, mass_ref, wide_ref, pick, chunk):
    parts = []
    for u in range(SPREAD // LANES):
        start = pl.multiple_of(chunk * SPREAD + u * LANES, LANES)
        rows = jnp.concatenate(
            [
                state_ref[:, pl.ds(start, LANES)],
                mass_ref[pl.ds(chunk * (SPREAD // LANES) + u, 1), :],
                jnp.zeros((1, LANES), jnp.float32),
            ],
            axis=0,
        )
        parts.append(pieces(rows).T)
    columns = jnp.concatenate(parts, axis=0).astype(jnp.bfloat16)
    wide = jnp.dot(columns, pick, preferred_element_type=jnp.float32)
    at = pl.ds(pl.multiple_of(chunk * SPREAD, SPREAD), SPREAD)
    for c in range(7):
        wide_ref[c, at, :] = wide[:, c * LANES : (c + 1) * LANES]


def tile_terms(active, wide_ref, stars):
    mine = [jnp.broadcast_to(active[c : c + 1, :], (8, LANES)) for c in range(6)]

    def body(step, totals):
        totals = list(totals)
        for u in range(UNROLL):
            at = pl.ds(pl.multiple_of((step * UNROLL + u) * 8, 8), 8)
            dx = [wide_ref[c, at, :] - mine[c] for c in range(3)]
            dv = [wide_ref[c, at, :] - mine[c] for c in range(3, 6)]
            raw = dx[0] * dx[0] + dx[1] * dx[1] + dx[2] * dx[2]
            weight = jnp.where(raw == 0.0, 0.0, wide_ref[6, at, :])
            inv = lax.rsqrt(raw + softening)
            square = inv * inv
            first = weight * inv
            third = first * square
            along = dx[0] * dv[0] + dx[1] * dv[1] + dx[2] * dv[2]
            ratio = (3.0 * along) * square
            for c in range(3):
                totals[c] = totals[c] + third * dx[c]
                totals[3 + c] = totals[3 + c] + third * (dv[c] - ratio * dx[c])
            totals[6] = totals[6] + first
        return tuple(totals)

    zero = jnp.zeros((8, LANES), jnp.float32)
    totals = lax.fori_loop(0, stars // (8 * UNROLL), body, (zero,) * 7)
    sums = [jnp.sum(t, axis=0, keepdims=True) for t in totals]
    return jnp.concatenate(sums[:6] + [-sums[6], jnp.zeros((1, LANES), jnp.float32)], axis=0)


def kernel(
    n_blk, n_grp, cap, state_in, mass_in, picks_in, counts_in, out_ref, pot_ref,
    state_ref, mass_ref, picks_ref, counts_ref, load_sem, wide_ref, part_ref, part_in, own_ref, own_in, sum_ref, sum_in, tot_ref, tot_in,
    part_s, part_r, own_s, own_r, sum_s, sum_r, tot_s, tot_r,
):
    blk, grp = lax.axis_index("blk"), lax.axis_index("grp")
    stars = state_ref.shape[1]
    size = LANES // cap
    tiles = n_blk // size
    tile, place = blk // size, blk % size
    hops = [(dt, dr) for dt in range(tiles) for dr in range(size)]

    def slot(dt, dr):
        return ((tile + dt) % tiles) * size + (place + dr) % size

    barrier = pltpu.get_barrier_semaphore()
    for d in range(1, n_grp):
        pl.semaphore_signal(barrier, inc=1, device_id=(blk, (grp + d) % n_grp), device_id_type=MESH)
    for dt, dr in hops[1:]:
        pl.semaphore_signal(barrier, inc=1, device_id=(slot(dt, dr), grp), device_id_type=MESH)

    loads = [
        pltpu.make_async_copy(src, dst, load_sem.at[i])
        for i, (src, dst) in enumerate(
            [(state_in, state_ref), (mass_in, mass_ref), (picks_in, picks_ref), (counts_in, counts_ref)]
        )
    ]
    for copy in loads:
        copy.start()
    for copy in loads:
        copy.wait()

    picks = jnp.concatenate([picks_ref[...] - grp * stars] * size, axis=1)
    lane = lax.broadcasted_iota(jnp.int32, (1, LANES), 1)
    picks = jnp.where(lane // cap == place, picks, -1)
    depth = 512
    row = lax.broadcasted_iota(jnp.int32, (depth, LANES), 0)
    found = jnp.zeros((18, LANES), jnp.float32)
    for k in range(stars // depth):
        hot = jnp.where(row + k * depth == picks, 1.0, 0.0).astype(jnp.bfloat16)
        rows = pieces(state_ref[:, k * depth : (k + 1) * depth]).astype(jnp.bfloat16)
        found = found + jnp.dot(rows, hot, preferred_element_type=jnp.float32)
    found = found[0:6] + found[6:12] + found[12:18]
    part_ref[...] = jnp.concatenate([found, jnp.zeros((2, LANES), jnp.float32)], axis=0)

    source = lax.broadcasted_iota(jnp.int32, (24, 7 * LANES), 0) % 8
    target = lax.broadcasted_iota(jnp.int32, (24, 7 * LANES), 1) // LANES
    pick = jnp.where(source == target, 1.0, 0.0).astype(jnp.bfloat16)
    chunks = stars // SPREAD

    @pl.loop(0, chunks // 2)
    def _(chunk):
        spread_chunk(state_ref, mass_ref, wide_ref, pick, chunk)

    pl.semaphore_wait(barrier, n_grp - 1 + n_blk - 1)

    def grp_copy(src, dst, send, recv, d):
        return pltpu.make_async_remote_copy(
            src_ref=src, dst_ref=dst.at[d - 1], send_sem=send.at[d - 1], recv_sem=recv.at[d - 1],
            device_id=(blk, (grp + d) % n_grp), device_id_type=MESH,
        )

    parts = [grp_copy(part_ref, part_in, part_s, part_r, d) for d in range(1, n_grp)]
    for copy in parts:
        copy.start()

    @pl.loop(chunks // 2, chunks)
    def _(chunk):
        spread_chunk(state_ref, mass_ref, wide_ref, pick, chunk)

    own = part_ref[...]
    for d, copy in enumerate(parts):
        copy.wait_recv()
        own = own + part_in[d]
    own_ref[...] = own

    shares = {}
    for dt, dr in hops[1:]:
        shares[dt, dr] = pltpu.make_async_remote_copy(
            src_ref=own_ref, dst_ref=own_in.at[dt * size + dr], send_sem=own_s.at[dt * size + dr],
            recv_sem=own_r.at[dt * size + dr], device_id=(slot(dt, dr), grp), device_id_type=MESH,
        )
        shares[dt, dr].start()

    results = {}
    for dt in range(tiles):
        active = own if dt == 0 else None
        for dr in range(size):
            if (dt, dr) != (0, 0):
                shares[dt, dr].wait_recv()
                got = own_in[dt * size + dr]
                active = got if active is None else active + got
        terms = tile_terms(active, wide_ref, stars)
        sum_ref[dt] = terms
        for dr in range(size):
            if (dt, dr) != (0, 0):
                results[dt, dr] = pltpu.make_async_remote_copy(
                    src_ref=sum_ref.at[dt], dst_ref=sum_in.at[dt * size + dr], send_sem=sum_s.at[dt * size + dr],
                    recv_sem=sum_r.at[dt * size + dr], device_id=(slot(tiles - dt, dr), grp), device_id_type=MESH,
                )
                results[dt, dr].start()

    total = sum_ref[0]
    for dt, dr in hops[1:]:
        results[dt, dr].wait_recv()
        total = total + sum_in[dt * size + dr]
    tot_ref[...] = total
    totals = [grp_copy(tot_ref, tot_in, tot_s, tot_r, d) for d in range(1, n_grp)]
    for copy in totals:
        copy.start()
    for d, copy in enumerate(totals):
        copy.wait_recv()
        total = total + tot_in[d]

    total = pltpu.roll(total, ((size - place) % size) * cap, 1)
    total = jnp.where(lane < counts_ref[0], total, 0.0)
    out_ref[...] = total[0:6, 0:cap]
    pot_ref[...] = total[6:7, 0:cap]

    for copy in parts + list(shares.values()) + list(results.values()) + totals:
        copy.wait_send()


def solution(mesh):
    n_blk, n_grp = mesh.shape["blk"], mesh.shape["grp"]

    def on_device(state, mass, active_index, counts):
        stars, cap = state.shape[1], active_index.shape[1]
        f32 = jnp.float32
        tile = (8, LANES)
        sems = pltpu.SemaphoreType.DMA
        vmem = pl.BlockSpec(memory_space=pltpu.VMEM)
        out, pot = pl.pallas_call(
            functools.partial(kernel, n_blk, n_grp, cap),
            out_shape=(jax.ShapeDtypeStruct((6, cap), f32), jax.ShapeDtypeStruct((1, cap), f32)),
            in_specs=[pl.BlockSpec(memory_space=pltpu.HBM)] * 4,
            out_specs=(vmem, vmem),
            scratch_shapes=[
                pltpu.VMEM((6, stars), f32),
                pltpu.VMEM((stars // LANES, LANES), f32),
                pltpu.VMEM((1, cap), jnp.int32),
                pltpu.SMEM((1,), jnp.int32),
                sems((4,)),
                pltpu.VMEM((7, stars, LANES), f32),
                pltpu.VMEM(tile, f32),
                pltpu.VMEM((n_grp - 1, *tile), f32),
                pltpu.VMEM(tile, f32),
                pltpu.VMEM((n_blk, *tile), f32),
                pltpu.VMEM((n_blk * cap // LANES, *tile), f32),
                pltpu.VMEM((n_blk, *tile), f32),
                pltpu.VMEM(tile, f32),
                pltpu.VMEM((n_grp - 1, *tile), f32),
                sems((n_grp - 1,)), sems((n_grp - 1,)),
                sems((n_blk,)), sems((n_blk,)),
                sems((n_blk,)), sems((n_blk,)),
                sems((n_grp - 1,)), sems((n_grp - 1,)),
            ],
            compiler_params=pltpu.CompilerParams(
                collective_id=0, has_side_effects=True, vmem_limit_bytes=67043328
            ),
        )(state, mass.reshape(stars // LANES, LANES), active_index, counts)
        return out, pot.reshape(cap)

    placed = (P(None, ("blk", "grp")), P(("blk", "grp")), P("blk", None), P("blk"))
    return jax.shard_map(
        on_device, mesh=mesh, in_specs=placed, out_specs=(P(None, "blk"), P("blk")), check_vma=False
    )
```

```python
import functools

import jax
import jax.numpy as jnp
from jax import lax
from jax.experimental import pallas as pl
from jax.experimental.pallas import tpu as pltpu
from jax.sharding import PartitionSpec as P

softening = 0.001
LANES = 128
MESH = pl.DeviceIdType.MESH
UNROLL = 8
SPREAD = 512


def pieces(rows):
    out = []
    for _ in range(3):
        piece = rows.astype(jnp.bfloat16).astype(jnp.float32)
        out.append(piece)
        rows = rows - piece
    return jnp.concatenate(out, axis=0)


def spread_chunk(state_ref, mass_ref, wide_ref, pick, chunk):
    parts = []
    for u in range(SPREAD // LANES):
        start = pl.multiple_of(chunk * SPREAD + u * LANES, LANES)
        rows = jnp.concatenate(
            [
                state_ref[:, pl.ds(start, LANES)],
                mass_ref[pl.ds(chunk * (SPREAD // LANES) + u, 1), :],
                jnp.zeros((1, LANES), jnp.float32),
            ],
            axis=0,
        )
        parts.append(pieces(rows).T)
    columns = jnp.concatenate(parts, axis=0).astype(jnp.bfloat16)
    wide = jnp.dot(columns, pick, preferred_element_type=jnp.float32)
    at = pl.ds(pl.multiple_of(chunk * SPREAD, SPREAD), SPREAD)
    for c in range(7):
        wide_ref[c, at, :] = wide[:, c * LANES : (c + 1) * LANES]


def tile_terms(active, wide_ref, stars):
    mine = [jnp.broadcast_to(active[c : c + 1, :], (8, LANES)) for c in range(6)]

    def body(step, totals):
        totals = list(totals)
        for u in range(UNROLL):
            at = pl.ds(pl.multiple_of((step * UNROLL + u) * 8, 8), 8)
            dx = [wide_ref[c, at, :] - mine[c] for c in range(3)]
            dv = [wide_ref[c, at, :] - mine[c] for c in range(3, 6)]
            raw = dx[0] * dx[0] + dx[1] * dx[1] + dx[2] * dx[2]
            weight = jnp.where(raw == 0.0, 0.0, wide_ref[6, at, :])
            inv = lax.rsqrt(raw + softening)
            square = inv * inv
            first = weight * inv
            third = first * square
            along = dx[0] * dv[0] + dx[1] * dv[1] + dx[2] * dv[2]
            ratio = (3.0 * along) * square
            for c in range(3):
                totals[c] = totals[c] + third * dx[c]
                totals[3 + c] = totals[3 + c] + third * (dv[c] - ratio * dx[c])
            totals[6] = totals[6] + first
        return tuple(totals)

    zero = jnp.zeros((8, LANES), jnp.float32)
    totals = lax.fori_loop(0, stars // (8 * UNROLL), body, (zero,) * 7)
    sums = [jnp.sum(t, axis=0, keepdims=True) for t in totals]
    return jnp.concatenate(sums[:6] + [-sums[6], jnp.zeros((1, LANES), jnp.float32)], axis=0)


def kernel(
    n_blk, n_grp, cap, state_in, mass_in, picks_in, counts_ref, out_ref, pot_ref,
    state_ref, mass_ref, picks_ref, load_sem, wide_ref, part_ref, part_in, own_ref, own_in, sum_ref, sum_in, tot_ref, tot_in,
    part_s, part_r, own_s, own_r, sum_s, sum_r, tot_s, tot_r,
):
    blk, grp = lax.axis_index("blk"), lax.axis_index("grp")
    stars = state_ref.shape[1]
    size = LANES // cap
    tiles = n_blk // size
    tile, place = blk // size, blk % size
    hops = [(dt, dr) for dt in range(tiles) for dr in range(size)]

    def slot(dt, dr):
        return ((tile + dt) % tiles) * size + (place + dr) % size

    barrier = pltpu.get_barrier_semaphore()
    for d in range(1, n_grp):
        pl.semaphore_signal(barrier, inc=1, device_id=(blk, (grp + d) % n_grp), device_id_type=MESH)
    for dt, dr in hops[1:]:
        pl.semaphore_signal(barrier, inc=1, device_id=(slot(dt, dr), grp), device_id_type=MESH)

    loads = [
        pltpu.make_async_copy(src, dst, load_sem.at[i])
        for i, (src, dst) in enumerate(
            [(state_in, state_ref), (mass_in, mass_ref), (picks_in, picks_ref)]
        )
    ]
    for copy in loads:
        copy.start()
    for copy in loads:
        copy.wait()

    picks = jnp.concatenate([picks_ref[...] - grp * stars] * size, axis=1)
    lane = lax.broadcasted_iota(jnp.int32, (1, LANES), 1)
    picks = jnp.where(lane // cap == place, picks, -1)
    depth = 512
    row = lax.broadcasted_iota(jnp.int32, (depth, LANES), 0)
    found = jnp.zeros((18, LANES), jnp.float32)
    for k in range(stars // depth):
        hot = jnp.where(row + k * depth == picks, 1.0, 0.0).astype(jnp.bfloat16)
        rows = pieces(state_ref[:, k * depth : (k + 1) * depth]).astype(jnp.bfloat16)
        found = found + jnp.dot(rows, hot, preferred_element_type=jnp.float32)
    found = found[0:6] + found[6:12] + found[12:18]
    part_ref[...] = jnp.concatenate([found, jnp.zeros((2, LANES), jnp.float32)], axis=0)

    source = lax.broadcasted_iota(jnp.int32, (24, 7 * LANES), 0) % 8
    target = lax.broadcasted_iota(jnp.int32, (24, 7 * LANES), 1) // LANES
    pick = jnp.where(source == target, 1.0, 0.0).astype(jnp.bfloat16)
    chunks = stars // SPREAD

    @pl.loop(0, chunks // 2)
    def _(chunk):
        spread_chunk(state_ref, mass_ref, wide_ref, pick, chunk)

    pl.semaphore_wait(barrier, n_grp - 1 + n_blk - 1)

    def grp_copy(src, dst, send, recv, d):
        return pltpu.make_async_remote_copy(
            src_ref=src, dst_ref=dst.at[d - 1], send_sem=send.at[d - 1], recv_sem=recv.at[d - 1],
            device_id=(blk, (grp + d) % n_grp), device_id_type=MESH,
        )

    parts = [grp_copy(part_ref, part_in, part_s, part_r, d) for d in range(1, n_grp)]
    for copy in parts:
        copy.start()

    @pl.loop(chunks // 2, chunks)
    def _(chunk):
        spread_chunk(state_ref, mass_ref, wide_ref, pick, chunk)

    own = part_ref[...]
    for d, copy in enumerate(parts):
        copy.wait_recv()
        own = own + part_in[d]
    own_ref[...] = own

    shares = {}
    for dt, dr in hops[1:]:
        shares[dt, dr] = pltpu.make_async_remote_copy(
            src_ref=own_ref, dst_ref=own_in.at[dt * size + dr], send_sem=own_s.at[dt * size + dr],
            recv_sem=own_r.at[dt * size + dr], device_id=(slot(dt, dr), grp), device_id_type=MESH,
        )
        shares[dt, dr].start()

    results = {}
    for dt in range(tiles):
        active = own if dt == 0 else None
        for dr in range(size):
            if (dt, dr) != (0, 0):
                shares[dt, dr].wait_recv()
                got = own_in[dt * size + dr]
                active = got if active is None else active + got
        terms = tile_terms(active, wide_ref, stars)
        sum_ref[dt] = terms
        for dr in range(size):
            if (dt, dr) != (0, 0):
                results[dt, dr] = pltpu.make_async_remote_copy(
                    src_ref=sum_ref.at[dt], dst_ref=sum_in.at[dt * size + dr], send_sem=sum_s.at[dt * size + dr],
                    recv_sem=sum_r.at[dt * size + dr], device_id=(slot(tiles - dt, dr), grp), device_id_type=MESH,
                )
                results[dt, dr].start()

    total = sum_ref[0]
    for dt, dr in hops[1:]:
        results[dt, dr].wait_recv()
        total = total + sum_in[dt * size + dr]
    tot_ref[...] = total
    totals = [grp_copy(tot_ref, tot_in, tot_s, tot_r, d) for d in range(1, n_grp)]
    for copy in totals:
        copy.start()
    for d, copy in enumerate(totals):
        copy.wait_recv()
        total = total + tot_in[d]

    total = pltpu.roll(total, ((size - place) % size) * cap, 1)
    total = jnp.where(lane < counts_ref[0], total, 0.0)
    out_ref[...] = total[0:6, 0:cap]
    pot_ref[...] = total[6:7, 0:cap]

    for copy in parts + list(shares.values()) + list(results.values()) + totals:
        copy.wait_send()


def solution(mesh):
    n_blk, n_grp = mesh.shape["blk"], mesh.shape["grp"]

    def on_device(state, mass, active_index, counts):
        stars, cap = state.shape[1], active_index.shape[1]
        f32 = jnp.float32
        tile = (8, LANES)
        sems = pltpu.SemaphoreType.DMA
        vmem = pl.BlockSpec(memory_space=pltpu.VMEM)
        out, pot = pl.pallas_call(
            functools.partial(kernel, n_blk, n_grp, cap),
            out_shape=(jax.ShapeDtypeStruct((6, cap), f32), jax.ShapeDtypeStruct((1, cap), f32)),
            in_specs=[pl.BlockSpec(memory_space=pltpu.HBM)] * 3 + [pl.BlockSpec(memory_space=pltpu.SMEM)],
            out_specs=(vmem, vmem),
            scratch_shapes=[
                pltpu.VMEM((6, stars), f32),
                pltpu.VMEM((stars // LANES, LANES), f32),
                pltpu.VMEM((1, cap), jnp.int32),
                sems((3,)),
                pltpu.VMEM((7, stars, LANES), f32),
                pltpu.VMEM(tile, f32),
                pltpu.VMEM((n_grp - 1, *tile), f32),
                pltpu.VMEM(tile, f32),
                pltpu.VMEM((n_blk, *tile), f32),
                pltpu.VMEM((n_blk * cap // LANES, *tile), f32),
                pltpu.VMEM((n_blk, *tile), f32),
                pltpu.VMEM(tile, f32),
                pltpu.VMEM((n_grp - 1, *tile), f32),
                sems((n_grp - 1,)), sems((n_grp - 1,)),
                sems((n_blk,)), sems((n_blk,)),
                sems((n_blk,)), sems((n_blk,)),
                sems((n_grp - 1,)), sems((n_grp - 1,)),
            ],
            compiler_params=pltpu.CompilerParams(
                collective_id=0, has_side_effects=True, vmem_limit_bytes=40 * 1024 * 1024
            ),
        )(*(
            pltpu.with_memory_space_constraint(x, pltpu.HBM)
            for x in (state, mass.reshape(stars // LANES, LANES), active_index)
        ), counts)
        return out, pot.reshape(cap)

    placed = (P(None, ("blk", "grp")), P(("blk", "grp")), P("blk", None), P("blk"))
    return jax.shard_map(
        on_device, mesh=mesh, in_specs=placed, out_specs=(P(None, "blk"), P("blk")), check_vma=False
    )
```

```python
import functools

import jax
import jax.numpy as jnp
from jax import lax
from jax.experimental import pallas as pl
from jax.experimental.pallas import tpu as pltpu
from jax.sharding import PartitionSpec as P

softening = 0.001
LANES = 128
MESH = pl.DeviceIdType.MESH
UNROLL = 8
SPREAD = 512


def pieces(rows):
    out = []
    for _ in range(3):
        piece = rows.astype(jnp.bfloat16).astype(jnp.float32)
        out.append(piece)
        rows = rows - piece
    return jnp.concatenate(out, axis=0)


def spread_chunk(state_ref, mass_ref, wide_ref, pick, chunk):
    parts = []
    for u in range(SPREAD // LANES):
        start = pl.multiple_of(chunk * SPREAD + u * LANES, LANES)
        rows = jnp.concatenate(
            [
                state_ref[:, pl.ds(start, LANES)],
                mass_ref[pl.ds(chunk * (SPREAD // LANES) + u, 1), :],
                jnp.zeros((1, LANES), jnp.float32),
            ],
            axis=0,
        )
        parts.append(pieces(rows).T)
    columns = jnp.concatenate(parts, axis=0).astype(jnp.bfloat16)
    wide = jnp.dot(columns, pick, preferred_element_type=jnp.float32)
    at = pl.ds(pl.multiple_of(chunk * SPREAD, SPREAD), SPREAD)
    for c in range(7):
        wide_ref[c, at, :] = wide[:, c * LANES : (c + 1) * LANES]


def turned(x, cap):
    return [x] + [pltpu.roll(x, k * cap, 1) for k in range(1, LANES // cap)]


def by_block(rows, cap):
    block = lax.broadcasted_iota(jnp.int32, rows[0].shape, 1) // cap
    out = rows[0]
    for b in range(1, len(rows)):
        out = jnp.where(block == b, rows[b], out)
    return out


def tile_terms(packed, wide_ref, stars, cap):
    size = LANES // cap
    high = 8 // size
    moved = turned(packed, cap)
    mine = []
    for c in range(6):
        rows = [moved[(b - c % size) % size][b * high + c // size :][:1] for b in range(size)]
        mine.append(jnp.broadcast_to(by_block(rows, cap), (8, LANES)))

    def body(step, totals):
        totals = list(totals)
        for u in range(UNROLL):
            at = pl.ds(pl.multiple_of((step * UNROLL + u) * 8, 8), 8)
            dx = [wide_ref[c, at, :] - mine[c] for c in range(3)]
            dv = [wide_ref[c, at, :] - mine[c] for c in range(3, 6)]
            raw = dx[0] * dx[0] + dx[1] * dx[1] + dx[2] * dx[2]
            weight = jnp.where(raw == 0.0, 0.0, wide_ref[6, at, :])
            inv = lax.rsqrt(raw + softening)
            square = inv * inv
            first = weight * inv
            third = first * square
            along = dx[0] * dv[0] + dx[1] * dv[1] + dx[2] * dv[2]
            ratio = (3.0 * along) * square
            for c in range(3):
                totals[c] = totals[c] + third * dx[c]
                totals[3 + c] = totals[3 + c] + third * (dv[c] - ratio * dx[c])
            totals[6] = totals[6] + first
        return tuple(totals)

    zero = jnp.zeros((8, LANES), jnp.float32)
    totals = lax.fori_loop(0, stars // (8 * UNROLL), body, (zero,) * 7)
    sums = [jnp.sum(t, axis=0, keepdims=True) for t in totals]
    moved = turned(jnp.concatenate(sums[:6] + [-sums[6], jnp.zeros((1, LANES), jnp.float32)], axis=0), cap)
    rows = []
    for b in range(size):
        for r in range(high):
            rows.append(by_block([moved[(q - b) % size][r * size + q :][:1] for q in range(size)], cap))
    return jnp.concatenate(rows, axis=0)


def kernel(
    n_blk, n_grp, cap, state_in, mass_in, picks_in, counts_ref, out_ref, pot_ref,
    state_ref, mass_ref, picks_ref, load_sem, wide_ref, part_ref, own_in, sum_ref, sum_in,
    own_s, own_r, sum_s, sum_r,
):
    blk, grp = lax.axis_index("blk"), lax.axis_index("grp")
    stars = state_ref.shape[1]
    size = LANES // cap
    high = 8 // size
    tiles = n_blk // size
    group = size * n_grp
    everyone = n_blk * n_grp
    tile, place = blk // size, blk % size
    me = blk * n_grp + grp

    def ahead(i):
        dt, dr, dg = i // group, (i % group) // n_grp, i % n_grp
        return ((tile + dt) % tiles) * size + (place + dr) % size, (grp + dg) % n_grp

    def behind(i):
        dt, dr, dg = i // group, (i % group) // n_grp, i % n_grp
        return ((tile + tiles - dt) % tiles) * size + (place + size - dr) % size, (grp + n_grp - dg) % n_grp

    barrier = pltpu.get_barrier_semaphore()

    @pl.loop(1, everyone)
    def _(i):
        pl.semaphore_signal(barrier, inc=1, device_id=ahead(everyone - i), device_id_type=MESH)

    loads = [
        pltpu.make_async_copy(src, dst, load_sem.at[i])
        for i, (src, dst) in enumerate(
            [(state_in, state_ref), (mass_in, mass_ref), (picks_in, picks_ref)]
        )
    ]
    for copy in loads:
        copy.start()
    for copy in loads:
        copy.wait()

    picks = jnp.concatenate([picks_ref[...] - grp * stars] * size, axis=1)
    depth = 512
    row = lax.broadcasted_iota(jnp.int32, (depth, LANES), 0)
    found = jnp.zeros((18, LANES), jnp.float32)
    for k in range(stars // depth):
        hot = jnp.where(row + k * depth == picks, 1.0, 0.0).astype(jnp.bfloat16)
        rows = pieces(state_ref[:, k * depth : (k + 1) * depth]).astype(jnp.bfloat16)
        found = found + jnp.dot(rows, hot, preferred_element_type=jnp.float32)
    found = found[0:6] + found[6:12] + found[12:18]
    found = jnp.concatenate([found, jnp.zeros((2, LANES), jnp.float32)], axis=0)
    part = jnp.concatenate(
        [by_block([found[r * size + q :][:1] for q in range(size)], cap) for r in range(high)], axis=0
    )
    part_ref[...] = part

    source = lax.broadcasted_iota(jnp.int32, (24, 7 * LANES), 0) % 8
    target = lax.broadcasted_iota(jnp.int32, (24, 7 * LANES), 1) // LANES
    pick = jnp.where(source == target, 1.0, 0.0).astype(jnp.bfloat16)
    chunks = stars // SPREAD

    @pl.loop(0, chunks // 2)
    def _(chunk):
        spread_chunk(state_ref, mass_ref, wide_ref, pick, chunk)

    pl.semaphore_wait(barrier, everyone - 1)

    def share(i):
        return pltpu.make_async_remote_copy(
            src_ref=part_ref, dst_ref=own_in.at[i], send_sem=own_s.at[i], recv_sem=own_r.at[i],
            device_id=ahead(i), device_id_type=MESH,
        )

    def give(i):
        return pltpu.make_async_remote_copy(
            src_ref=sum_ref.at[i // group, (i % group) // n_grp], dst_ref=sum_in.at[me], send_sem=sum_s.at[i],
            recv_sem=sum_r.at[me], device_id=behind(i), device_id_type=MESH,
        )

    def take(i):
        there = behind(i)
        at = there[0] * n_grp + there[1]
        return pltpu.make_async_remote_copy(
            src_ref=part_ref, dst_ref=sum_in.at[at], send_sem=sum_s.at[i], recv_sem=sum_r.at[at],
            device_id=there, device_id_type=MESH,
        )

    @pl.loop(1, everyone)
    def _(i):
        share(i).start()

    @pl.loop(chunks // 2, chunks)
    def _(chunk):
        spread_chunk(state_ref, mass_ref, wide_ref, pick, chunk)

    for dt in range(tiles):
        first = dt * group + (dt == 0)

        @pl.loop(first, (dt + 1) * group)
        def _(i):
            share(i).wait_recv()

        packed = []
        for dr in range(size):
            slot = part if dt == 0 and dr == 0 else own_in[dt * group + dr * n_grp]
            for dg in range(1, n_grp):
                slot = slot + own_in[dt * group + dr * n_grp + dg]
            packed.append(slot)
        terms = tile_terms(jnp.concatenate(packed, axis=0), wide_ref, stars, cap)
        for dr in range(size):
            sum_ref[dt, dr] = terms[dr * high : (dr + 1) * high]
        if dt == 0:
            sum_in[me] = terms[:high]

        @pl.loop(first, (dt + 1) * group)
        def _(i):
            give(i).start()

    @pl.loop(1, everyone)
    def _(i):
        take(i).wait_recv()

    total = sum_in[0]
    for k in range(1, everyone):
        total = total + sum_in[k]
    moved = turned(total, cap)
    rows = [moved[(size - c % size) % size][c // size :][:1, :cap] for c in range(7)]
    live = lax.broadcasted_iota(jnp.int32, (1, cap), 1) < counts_ref[0]
    out_ref[...] = jnp.where(live, jnp.concatenate(rows[:6], axis=0), 0.0)
    pot_ref[...] = jnp.where(live, rows[6], 0.0)

    @pl.loop(1, everyone)
    def _(i):
        share(i).wait_send()
        give(i).wait_send()


def solution(mesh):
    n_blk, n_grp = mesh.shape["blk"], mesh.shape["grp"]

    def on_device(state, mass, active_index, counts):
        stars, cap = state.shape[1], active_index.shape[1]
        f32 = jnp.float32
        tile = (8 * cap // LANES, LANES)
        everyone = n_blk * n_grp
        sems = pltpu.SemaphoreType.DMA
        vmem = pl.BlockSpec(memory_space=pltpu.VMEM)
        out, pot = pl.pallas_call(
            functools.partial(kernel, n_blk, n_grp, cap),
            out_shape=(jax.ShapeDtypeStruct((6, cap), f32), jax.ShapeDtypeStruct((1, cap), f32)),
            in_specs=[pl.BlockSpec(memory_space=pltpu.HBM)] * 3 + [pl.BlockSpec(memory_space=pltpu.SMEM)],
            out_specs=(vmem, vmem),
            scratch_shapes=[
                pltpu.VMEM((6, stars), f32),
                pltpu.VMEM((stars // LANES, LANES), f32),
                pltpu.VMEM((1, cap), jnp.int32),
                sems((3,)),
                pltpu.VMEM((7, stars, LANES), f32),
                pltpu.VMEM(tile, f32),
                pltpu.VMEM((everyone, *tile), f32),
                pltpu.VMEM((n_blk * cap // LANES, LANES // cap, *tile), f32),
                pltpu.VMEM((everyone, *tile), f32),
                sems((everyone,)), sems((everyone,)), sems((everyone,)), sems((everyone,)),
            ],
            compiler_params=pltpu.CompilerParams(
                collective_id=0, has_side_effects=True, vmem_limit_bytes=40 * 1024 * 1024
            ),
        )(*(
            pltpu.with_memory_space_constraint(x, pltpu.HBM)
            for x in (state, mass.reshape(stars // LANES, LANES), active_index)
        ), counts)
        return out, pot.reshape(cap)

    placed = (P(None, ("blk", "grp")), P(("blk", "grp")), P("blk", None), P("blk"))
    return jax.shard_map(
        on_device, mesh=mesh, in_specs=placed, out_specs=(P(None, "blk"), P("blk")), check_vma=False
    )
```

```python
import functools

import jax
import jax.numpy as jnp
from jax import lax
from jax.experimental import pallas as pl
from jax.experimental.pallas import tpu as pltpu
from jax.sharding import PartitionSpec as P

softening = 0.001
LANES = 128
MESH = pl.DeviceIdType.MESH
UNROLL = 8
SPREAD = 512


def pieces(rows):
    out = []
    for _ in range(3):
        piece = rows.astype(jnp.bfloat16).astype(jnp.float32)
        out.append(piece)
        rows = rows - piece
    return jnp.concatenate(out, axis=0)


def spread_chunk(state_ref, mass_ref, wide_ref, pick, chunk):
    parts = []
    for u in range(SPREAD // LANES):
        start = pl.multiple_of(chunk * SPREAD + u * LANES, LANES)
        rows = jnp.concatenate(
            [
                state_ref[:, pl.ds(start, LANES)],
                mass_ref[pl.ds(chunk * (SPREAD // LANES) + u, 1), :],
                jnp.zeros((1, LANES), jnp.float32),
            ],
            axis=0,
        )
        parts.append(pieces(rows).T)
    columns = jnp.concatenate(parts, axis=0).astype(jnp.bfloat16)
    wide = jnp.dot(columns, pick, preferred_element_type=jnp.float32)
    at = pl.ds(pl.multiple_of(chunk * SPREAD, SPREAD), SPREAD)
    for c in range(7):
        wide_ref[c, at, :] = wide[:, c * LANES : (c + 1) * LANES]


def turned(x, cap):
    return [x] + [pltpu.roll(x, k * cap, 1) for k in range(1, LANES // cap)]


def by_block(rows, cap):
    block = lax.broadcasted_iota(jnp.int32, rows[0].shape, 1) // cap
    out = rows[0]
    for b in range(1, len(rows)):
        out = jnp.where(block == b, rows[b], out)
    return out


def tile_terms(packed, wide_ref, stars, cap):
    size = LANES // cap
    high = 8 // size
    moved = turned(packed, cap)
    mine = []
    for c in range(6):
        rows = [moved[(b - c % size) % size][b * high + c // size :][:1] for b in range(size)]
        mine.append(jnp.broadcast_to(by_block(rows, cap), (8, LANES)))

    def body(step, totals):
        totals = list(totals)
        for u in range(UNROLL):
            at = pl.ds(pl.multiple_of((step * UNROLL + u) * 8, 8), 8)
            dx = [wide_ref[c, at, :] - mine[c] for c in range(3)]
            dv = [wide_ref[c, at, :] - mine[c] for c in range(3, 6)]
            raw = dx[0] * dx[0] + dx[1] * dx[1] + dx[2] * dx[2]
            weight = jnp.where(raw == 0.0, 0.0, wide_ref[6, at, :])
            inv = lax.rsqrt(raw + softening)
            square = inv * inv
            first = weight * inv
            third = first * square
            along = dx[0] * dv[0] + dx[1] * dv[1] + dx[2] * dv[2]
            ratio = (3.0 * along) * square
            for c in range(3):
                totals[c] = totals[c] + third * dx[c]
                totals[3 + c] = totals[3 + c] + third * (dv[c] - ratio * dx[c])
            totals[6] = totals[6] + first
        return tuple(totals)

    zero = jnp.zeros((8, LANES), jnp.float32)
    totals = lax.fori_loop(0, stars // (8 * UNROLL), body, (zero,) * 7)
    sums = [jnp.sum(t, axis=0, keepdims=True) for t in totals]
    moved = turned(jnp.concatenate(sums[:6] + [-sums[6], jnp.zeros((1, LANES), jnp.float32)], axis=0), cap)
    rows = []
    for b in range(size):
        for r in range(high):
            rows.append(by_block([moved[(q - b) % size][r * size + q :][:1] for q in range(size)], cap))
    return jnp.concatenate(rows, axis=0)


def kernel(
    n_blk, n_grp, cap, state_in, mass_in, picks_in, counts_ref, out_ref, pot_ref,
    state_ref, mass_ref, picks_ref, load_sem, wide_ref, part_ref, own_in, list_ref, list_in, sum_ref, sum_in,
    own_s, own_r, list_s, list_r, sum_s, sum_r,
):
    blk, grp = lax.axis_index("blk"), lax.axis_index("grp")
    stars = state_ref.shape[1]
    size = LANES // cap
    high = 8 // size
    tiles = n_blk // size
    group = size * n_grp
    everyone = n_blk * n_grp
    tile, place = blk // size, blk % size
    me = blk * n_grp + grp

    def ahead(i):
        dt, dr, dg = i // group, (i % group) // n_grp, i % n_grp
        return ((tile + dt) % tiles) * size + (place + dr) % size, (grp + dg) % n_grp

    def behind(i):
        dt, dr, dg = i // group, (i % group) // n_grp, i % n_grp
        return ((tile + tiles - dt) % tiles) * size + (place + size - dr) % size, (grp + n_grp - dg) % n_grp

    barrier = pltpu.get_barrier_semaphore()

    for dt in range(1, tiles):
        pl.semaphore_signal(barrier, inc=1, device_id=ahead(dt * group), device_id_type=MESH)

    @pl.loop(1, group)
    def _(i):
        pl.semaphore_signal(barrier, inc=1, device_id=ahead(group - i), device_id_type=MESH)

    loads = [
        pltpu.make_async_copy(src, dst, load_sem.at[i])
        for i, (src, dst) in enumerate(
            [(state_in, state_ref), (mass_in, mass_ref), (picks_in, picks_ref)]
        )
    ]
    for copy in loads:
        copy.start()
    for copy in loads:
        copy.wait()

    picks = jnp.concatenate([picks_ref[...] - grp * stars] * size, axis=1)
    depth = 512
    row = lax.broadcasted_iota(jnp.int32, (depth, LANES), 0)
    found = jnp.zeros((18, LANES), jnp.float32)
    for k in range(stars // depth):
        hot = jnp.where(row + k * depth == picks, 1.0, 0.0).astype(jnp.bfloat16)
        rows = pieces(state_ref[:, k * depth : (k + 1) * depth]).astype(jnp.bfloat16)
        found = found + jnp.dot(rows, hot, preferred_element_type=jnp.float32)
    found = found[0:6] + found[6:12] + found[12:18]
    found = jnp.concatenate([found, jnp.zeros((2, LANES), jnp.float32)], axis=0)
    part = jnp.concatenate(
        [by_block([found[r * size + q :][:1] for q in range(size)], cap) for r in range(high)], axis=0
    )
    part_ref[...] = part

    source = lax.broadcasted_iota(jnp.int32, (24, 7 * LANES), 0) % 8
    target = lax.broadcasted_iota(jnp.int32, (24, 7 * LANES), 1) // LANES
    pick = jnp.where(source == target, 1.0, 0.0).astype(jnp.bfloat16)
    chunks = stars // SPREAD

    @pl.loop(0, chunks // 2)
    def _(chunk):
        spread_chunk(state_ref, mass_ref, wide_ref, pick, chunk)

    pl.semaphore_wait(barrier, group - 1 + tiles - 1)

    def share(i):
        return pltpu.make_async_remote_copy(
            src_ref=part_ref, dst_ref=own_in.at[i], send_sem=own_s.at[i], recv_sem=own_r.at[i],
            device_id=ahead(i), device_id_type=MESH,
        )

    def pass_on(dt):
        return pltpu.make_async_remote_copy(
            src_ref=list_ref, dst_ref=list_in.at[dt], send_sem=list_s.at[dt], recv_sem=list_r.at[dt],
            device_id=ahead(dt * group), device_id_type=MESH,
        )

    def give(i):
        return pltpu.make_async_remote_copy(
            src_ref=sum_ref.at[i // group, (i % group) // n_grp], dst_ref=sum_in.at[me], send_sem=sum_s.at[i],
            recv_sem=sum_r.at[me], device_id=behind(i), device_id_type=MESH,
        )

    def take(i):
        there = behind(i)
        at = there[0] * n_grp + there[1]
        return pltpu.make_async_remote_copy(
            src_ref=part_ref, dst_ref=sum_in.at[at], send_sem=sum_s.at[i], recv_sem=sum_r.at[at],
            device_id=there, device_id_type=MESH,
        )

    @pl.loop(1, group)
    def _(i):
        share(i).start()

    @pl.loop(chunks // 2, chunks)
    def _(chunk):
        spread_chunk(state_ref, mass_ref, wide_ref, pick, chunk)

    @pl.loop(1, group)
    def _(i):
        share(i).wait_recv()

    packed = []
    for dr in range(size):
        slot = part if dr == 0 else own_in[dr * n_grp]
        for dg in range(1, n_grp):
            slot = slot + own_in[dr * n_grp + dg]
        packed.append(slot)
    packed = jnp.concatenate(packed, axis=0)
    list_ref[...] = packed
    for dt in range(1, tiles):
        pass_on(dt).start()

    for dt in range(tiles):
        first = dt * group + (dt == 0)
        if dt > 0:
            pass_on(dt).wait_recv()
            packed = list_in[dt]
        terms = tile_terms(packed, wide_ref, stars, cap)
        for dr in range(size):
            sum_ref[dt, dr] = terms[dr * high : (dr + 1) * high]
        if dt == 0:
            sum_in[me] = terms[:high]

        @pl.loop(first, (dt + 1) * group)
        def _(i):
            give(i).start()

    @pl.loop(1, everyone)
    def _(i):
        take(i).wait_recv()

    total = sum_in[0]
    for k in range(1, everyone):
        total = total + sum_in[k]
    moved = turned(total, cap)
    rows = [moved[(size - c % size) % size][c // size :][:1, :cap] for c in range(7)]
    live = lax.broadcasted_iota(jnp.int32, (1, cap), 1) < counts_ref[0]
    out_ref[...] = jnp.where(live, jnp.concatenate(rows[:6], axis=0), 0.0)
    pot_ref[...] = jnp.where(live, rows[6], 0.0)

    @pl.loop(1, everyone)
    def _(i):
        give(i).wait_send()

    @pl.loop(1, group)
    def _(i):
        share(i).wait_send()

    for dt in range(1, tiles):
        pass_on(dt).wait_send()


def solution(mesh):
    n_blk, n_grp = mesh.shape["blk"], mesh.shape["grp"]

    def on_device(state, mass, active_index, counts):
        stars, cap = state.shape[1], active_index.shape[1]
        f32 = jnp.float32
        tile = (8 * cap // LANES, LANES)
        tiles = n_blk * cap // LANES
        near = n_grp * LANES // cap
        everyone = n_blk * n_grp
        sems = pltpu.SemaphoreType.DMA
        vmem = pl.BlockSpec(memory_space=pltpu.VMEM)
        out, pot = pl.pallas_call(
            functools.partial(kernel, n_blk, n_grp, cap),
            out_shape=(jax.ShapeDtypeStruct((6, cap), f32), jax.ShapeDtypeStruct((1, cap), f32)),
            in_specs=[pl.BlockSpec(memory_space=pltpu.HBM)] * 3 + [pl.BlockSpec(memory_space=pltpu.SMEM)],
            out_specs=(vmem, vmem),
            scratch_shapes=[
                pltpu.VMEM((6, stars), f32),
                pltpu.VMEM((stars // LANES, LANES), f32),
                pltpu.VMEM((1, cap), jnp.int32),
                sems((3,)),
                pltpu.VMEM((7, stars, LANES), f32),
                pltpu.VMEM(tile, f32),
                pltpu.VMEM((near, *tile), f32),
                pltpu.VMEM((8, LANES), f32),
                pltpu.VMEM((tiles, 8, LANES), f32),
                pltpu.VMEM((tiles, LANES // cap, *tile), f32),
                pltpu.VMEM((everyone, *tile), f32),
                sems((near,)), sems((near,)), sems((tiles,)), sems((tiles,)), sems((everyone,)), sems((everyone,)),
            ],
            compiler_params=pltpu.CompilerParams(
                collective_id=0, has_side_effects=True, vmem_limit_bytes=40 * 1024 * 1024
            ),
        )(*(
            pltpu.with_memory_space_constraint(x, pltpu.HBM)
            for x in (state, mass.reshape(stars // LANES, LANES), active_index)
        ), counts)
        return out, pot.reshape(cap)

    placed = (P(None, ("blk", "grp")), P(("blk", "grp")), P("blk", None), P("blk"))
    return jax.shard_map(
        on_device, mesh=mesh, in_specs=placed, out_specs=(P(None, "blk"), P("blk")), check_vma=False
    )
```

```python
import functools

import jax
import jax.numpy as jnp
from jax import lax
from jax.experimental import pallas as pl
from jax.experimental.pallas import tpu as pltpu
from jax.sharding import PartitionSpec as P

softening = 0.001
LANES = 128
MESH = pl.DeviceIdType.MESH
UNROLL = 8
SPREAD = 512


def pieces(rows):
    out = []
    for _ in range(3):
        piece = rows.astype(jnp.bfloat16).astype(jnp.float32)
        out.append(piece)
        rows = rows - piece
    return jnp.concatenate(out, axis=0)


def spread_chunk(state_ref, mass_ref, wide_ref, pick, chunk):
    parts = []
    for u in range(SPREAD // LANES):
        start = pl.multiple_of(chunk * SPREAD + u * LANES, LANES)
        rows = jnp.concatenate(
            [
                state_ref[:, pl.ds(start, LANES)],
                mass_ref[pl.ds(chunk * (SPREAD // LANES) + u, 1), :],
                jnp.zeros((1, LANES), jnp.float32),
            ],
            axis=0,
        )
        parts.append(pieces(rows).T)
    columns = jnp.concatenate(parts, axis=0).astype(jnp.bfloat16)
    wide = jnp.dot(columns, pick, preferred_element_type=jnp.float32)
    at = pl.ds(pl.multiple_of(chunk * SPREAD, SPREAD), SPREAD)
    for c in range(7):
        wide_ref[c, at, :] = wide[:, c * LANES : (c + 1) * LANES]


def turned(x, cap):
    return [x] + [pltpu.roll(x, k * cap, 1) for k in range(1, LANES // cap)]


def by_block(rows, cap):
    block = lax.broadcasted_iota(jnp.int32, rows[0].shape, 1) // cap
    out = rows[0]
    for b in range(1, len(rows)):
        out = jnp.where(block == b, rows[b], out)
    return out


def tile_terms(packed, wide_ref, begin, end, cap):
    size = LANES // cap
    high = 8 // size
    moved = turned(packed, cap)
    mine = []
    for c in range(6):
        rows = [moved[(b - c % size) % size][b * high + c // size :][:1] for b in range(size)]
        mine.append(jnp.broadcast_to(by_block(rows, cap), (8, LANES)))

    def body(step, totals):
        totals = list(totals)
        for u in range(UNROLL):
            at = pl.ds(pl.multiple_of((step * UNROLL + u) * 8, 8), 8)
            dx = [wide_ref[c, at, :] - mine[c] for c in range(3)]
            dv = [wide_ref[c, at, :] - mine[c] for c in range(3, 6)]
            raw = dx[0] * dx[0] + dx[1] * dx[1] + dx[2] * dx[2]
            weight = jnp.where(raw == 0.0, 0.0, wide_ref[6, at, :])
            inv = lax.rsqrt(raw + softening)
            square = inv * inv
            first = weight * inv
            third = first * square
            along = dx[0] * dv[0] + dx[1] * dv[1] + dx[2] * dv[2]
            ratio = (3.0 * along) * square
            for c in range(3):
                totals[c] = totals[c] + third * dx[c]
                totals[3 + c] = totals[3 + c] + third * (dv[c] - ratio * dx[c])
            totals[6] = totals[6] + first
        return tuple(totals)

    zero = jnp.zeros((8, LANES), jnp.float32)
    totals = lax.fori_loop(begin // (8 * UNROLL), end // (8 * UNROLL), body, (zero,) * 7)
    sums = [jnp.sum(t, axis=0, keepdims=True) for t in totals]
    moved = turned(jnp.concatenate(sums[:6] + [-sums[6], jnp.zeros((1, LANES), jnp.float32)], axis=0), cap)
    rows = []
    for b in range(size):
        for r in range(high):
            rows.append(by_block([moved[(q - b) % size][r * size + q :][:1] for q in range(size)], cap))
    return jnp.concatenate(rows, axis=0)


def each(first, last, do):
    if last - first <= 32:
        for i in range(first, last):
            do(i)
    else:
        pl.loop(first, last)(do)


def kernel(
    n_blk, n_grp, cap, state_in, mass_in, picks_in, counts_ref, out_ref, pot_ref,
    state_ref, mass_ref, picks_ref, load_sem, wide_ref, part_ref, own_in, list_ref, list_in, sum_ref, sum_in,
    own_s, own_r, list_s, list_r, sum_s, sum_r,
):
    blk, grp = lax.axis_index("blk"), lax.axis_index("grp")
    stars = state_ref.shape[1]
    size = LANES // cap
    high = 8 // size
    tiles = n_blk // size
    group = size * n_grp
    everyone = n_blk * n_grp
    tile, place = blk // size, blk % size
    me = blk * n_grp + grp

    def ahead(i):
        dt, dr, dg = i // group, (i % group) // n_grp, i % n_grp
        return ((tile + dt) % tiles) * size + (place + dr) % size, (grp + dg) % n_grp

    def behind(i):
        dt, dr, dg = i // group, (i % group) // n_grp, i % n_grp
        return ((tile + tiles - dt) % tiles) * size + (place + size - dr) % size, (grp + n_grp - dg) % n_grp

    barrier = pltpu.get_barrier_semaphore()

    for dt in range(1, tiles):
        pl.semaphore_signal(barrier, inc=1, device_id=ahead(dt * group), device_id_type=MESH)

    @pl.loop(1, group)
    def _(i):
        pl.semaphore_signal(barrier, inc=1, device_id=ahead(group - i), device_id_type=MESH)

    loads = [
        pltpu.make_async_copy(src, dst, load_sem.at[i])
        for i, (src, dst) in enumerate(
            [(state_in, state_ref), (mass_in, mass_ref), (picks_in, picks_ref)]
        )
    ]
    for copy in loads:
        copy.start()
    for copy in loads:
        copy.wait()

    picks = jnp.concatenate([picks_ref[...] - grp * stars] * size, axis=1)
    depth = 512
    row = lax.broadcasted_iota(jnp.int32, (depth, LANES), 0)
    found = jnp.zeros((18, LANES), jnp.float32)
    for k in range(stars // depth):
        hot = jnp.where(row + k * depth == picks, 1.0, 0.0).astype(jnp.bfloat16)
        rows = pieces(state_ref[:, k * depth : (k + 1) * depth]).astype(jnp.bfloat16)
        found = found + jnp.dot(rows, hot, preferred_element_type=jnp.float32)
    found = found[0:6] + found[6:12] + found[12:18]
    found = jnp.concatenate([found, jnp.zeros((2, LANES), jnp.float32)], axis=0)
    part = jnp.concatenate(
        [by_block([found[r * size + q :][:1] for q in range(size)], cap) for r in range(high)], axis=0
    )
    part_ref[...] = part

    source = lax.broadcasted_iota(jnp.int32, (24, 7 * LANES), 0) % 8
    target = lax.broadcasted_iota(jnp.int32, (24, 7 * LANES), 1) // LANES
    pick = jnp.where(source == target, 1.0, 0.0).astype(jnp.bfloat16)
    chunks = stars // SPREAD

    @pl.loop(0, chunks // 2)
    def _(chunk):
        spread_chunk(state_ref, mass_ref, wide_ref, pick, chunk)

    pl.semaphore_wait(barrier, group - 1 + tiles - 1)

    def share(i):
        return pltpu.make_async_remote_copy(
            src_ref=part_ref, dst_ref=own_in.at[i], send_sem=own_s.at[i], recv_sem=own_r.at[i],
            device_id=ahead(i), device_id_type=MESH,
        )

    def pass_on(dt):
        return pltpu.make_async_remote_copy(
            src_ref=list_ref, dst_ref=list_in.at[dt], send_sem=list_s.at[dt], recv_sem=list_r.at[dt],
            device_id=ahead(dt * group), device_id_type=MESH,
        )

    def give(i):
        return pltpu.make_async_remote_copy(
            src_ref=sum_ref.at[i // group, (i % group) // n_grp], dst_ref=sum_in.at[me], send_sem=sum_s.at[i],
            recv_sem=sum_r.at[me], device_id=behind(i), device_id_type=MESH,
        )

    def take(i):
        there = behind(i)
        at = there[0] * n_grp + there[1]
        return pltpu.make_async_remote_copy(
            src_ref=part_ref, dst_ref=sum_in.at[at], send_sem=sum_s.at[i], recv_sem=sum_r.at[at],
            device_id=there, device_id_type=MESH,
        )

    each(1, group, lambda i: share(i).start())

    @pl.loop(chunks // 2, chunks)
    def _(chunk):
        spread_chunk(state_ref, mass_ref, wide_ref, pick, chunk)

    each(1, group, lambda i: share(i).wait_recv())

    packed = []
    for dr in range(size):
        slot = part if dr == 0 else own_in[dr * n_grp]
        for dg in range(1, n_grp):
            slot = slot + own_in[dr * n_grp + dg]
        packed.append(slot)
    packed = jnp.concatenate(packed, axis=0)
    list_ref[...] = packed
    for dt in range(1, tiles):
        pass_on(dt).start()

    def hand_out(dt, terms):
        for dr in range(size):
            sum_ref[dt, dr] = terms[dr * high : (dr + 1) * high]

        each(dt * group + (dt == 0), (dt + 1) * group, lambda i: give(i).start())

    most = stars // 4 * 3
    terms = tile_terms(packed, wide_ref, 0, most, cap)
    for dt in range(1, tiles):
        pass_on(dt).wait_recv()
        hand_out(dt, tile_terms(list_in[dt], wide_ref, 0, stars, cap))
    terms = terms + tile_terms(packed, wide_ref, most, stars, cap)
    sum_in[me] = terms[:high]
    hand_out(0, terms)

    each(1, everyone, lambda i: take(i).wait_recv())

    total = sum_in[0]
    for k in range(1, everyone):
        total = total + sum_in[k]
    moved = turned(total, cap)
    rows = [moved[(size - c % size) % size][c // size :][:1, :cap] for c in range(7)]
    live = lax.broadcasted_iota(jnp.int32, (1, cap), 1) < counts_ref[0]
    out_ref[...] = jnp.where(live, jnp.concatenate(rows[:6], axis=0), 0.0)
    pot_ref[...] = jnp.where(live, rows[6], 0.0)

    each(1, everyone, lambda i: give(i).wait_send())

    each(1, group, lambda i: share(i).wait_send())

    for dt in range(1, tiles):
        pass_on(dt).wait_send()


def solution(mesh):
    n_blk, n_grp = mesh.shape["blk"], mesh.shape["grp"]

    def on_device(state, mass, active_index, counts):
        stars, cap = state.shape[1], active_index.shape[1]
        f32 = jnp.float32
        tile = (8 * cap // LANES, LANES)
        tiles = n_blk * cap // LANES
        near = n_grp * LANES // cap
        everyone = n_blk * n_grp
        sems = pltpu.SemaphoreType.DMA
        vmem = pl.BlockSpec(memory_space=pltpu.VMEM)
        out, pot = pl.pallas_call(
            functools.partial(kernel, n_blk, n_grp, cap),
            out_shape=(jax.ShapeDtypeStruct((6, cap), f32), jax.ShapeDtypeStruct((1, cap), f32)),
            in_specs=[pl.BlockSpec(memory_space=pltpu.HBM)] * 3 + [pl.BlockSpec(memory_space=pltpu.SMEM)],
            out_specs=(vmem, vmem),
            scratch_shapes=[
                pltpu.VMEM((6, stars), f32),
                pltpu.VMEM((stars // LANES, LANES), f32),
                pltpu.VMEM((1, cap), jnp.int32),
                sems((3,)),
                pltpu.VMEM((7, stars, LANES), f32),
                pltpu.VMEM(tile, f32),
                pltpu.VMEM((near, *tile), f32),
                pltpu.VMEM((8, LANES), f32),
                pltpu.VMEM((tiles, 8, LANES), f32),
                pltpu.VMEM((tiles, LANES // cap, *tile), f32),
                pltpu.VMEM((everyone, *tile), f32),
                sems((near,)), sems((near,)), sems((tiles,)), sems((tiles,)), sems((everyone,)), sems((everyone,)),
            ],
            compiler_params=pltpu.CompilerParams(
                collective_id=0, has_side_effects=True, vmem_limit_bytes=40 * 1024 * 1024
            ),
        )(*(
            pltpu.with_memory_space_constraint(x, pltpu.HBM)
            for x in (state, mass.reshape(stars // LANES, LANES), active_index)
        ), counts)
        return out, pot.reshape(cap)

    placed = (P(None, ("blk", "grp")), P(("blk", "grp")), P("blk", None), P("blk"))
    return jax.shard_map(
        on_device, mesh=mesh, in_specs=placed, out_specs=(P(None, "blk"), P("blk")), check_vma=False
    )
```
